1024 devices in a mesh: ctx: 128 (over y, x, core), head: 8 (over z).
Axes of the slice: x: 8, y: 8, z: 8, core: 2. Of those that a mesh axis runs over, the one named last changes fastest.
Arguments:
- queries: bfloat16 [32768, 4096], P('ctx', 'head'), may hold values from -5 to 5
- keys: bfloat16 [32768, 4096], P('ctx', 'head'), may hold values from -5 to 5
- values: bfloat16 [32768, 4096], P('ctx', 'head'), may hold values from -1300 to 1300
- gate_logits: bfloat16 [32768, 4096], P('ctx', 'head'), may hold values from -6 to 6
- norm_gain: float32 [4096], replicated, may hold values from 0.1 to 1.9
- out_weight: bfloat16 [4096, 6144], P(None, 'head'), may hold values from -0.09375 to 0.09375
- residual: bfloat16 [32768, 6144], P('ctx', 'head'), may hold values from -4 to 4
Outputs:
- layer_out: bfloat16 [32768, 6144], P('ctx', 'head')
The draws below stay inside these ranges and needn't reach their ends.
All inputs are finite; a program needn't handle non-finite values.
Results may differ from the reference program's by a relative error of at most 0.011.
Values may be sent and summed in bfloat16 or wider, within the bound.
No kernel may reach another device: no remote copies, remote signals or barrier semaphores. Data moves between devices by JAX's collectives and lax.ppermute only.
A program may use at most 64 MiB of HBM per device.

```python
import math
import jax
import jax.numpy as jnp
from jax import lax

D = 6144
HEAD_DIM = 128
HEADS = 32
BLOCK = 256
INNER = 4096
SEQ = 32768


def draw_values(key, part):
    base_key = jax.random.fold_in(key, 7)
    entry_key, row_key, jitter_key = jax.random.split(base_key, 3)
    column_head = jnp.arange(INNER) // HEAD_DIM
    position = column_head.astype(jnp.float32) / max(HEADS - 1, 1)
    jitter = jnp.exp(jax.random.uniform(jitter_key, (HEADS,), jnp.float32, -0.2, 0.2))[column_head]
    row_scale = jnp.exp(jax.random.uniform(row_key, (SEQ, 1), jnp.float32, 0.0, math.log(10.0)))
    entries = jnp.clip(jax.random.normal(entry_key, (SEQ, INNER), jnp.float32), -4.0, 4.0)
    column_scale = 10.0 ** position
    return (entries * column_scale[None, :] * jitter[None, :] * row_scale).astype(jnp.bfloat16)


def block_scale(rng, extent, cuts, least, largest):
    gain, own = 1.0, jax.random.fold_in(rng, 6)
    for axis_at, parts in cuts:
        heights = jnp.exp(jax.random.uniform(jax.random.fold_in(own, axis_at), (parts,), jnp.float32, least / len(cuts), largest / len(cuts)))
        gain = gain * jnp.repeat(heights, extent[axis_at] // parts).reshape([-1 if axis == axis_at else 1 for axis in range(len(extent))])
    return gain


def scatter_about(stream_key, extent, scale, most, pieces=(), kind=jnp.bfloat16):
    values = scale * jax.random.normal(stream_key, extent, jnp.float32)
    if pieces:
        values = values * block_scale(stream_key, extent, pieces, -0.22, 0.18)
    return jnp.clip(values, -most, most).astype(kind)


def setup_inputs(seed: int = 0) -> dict:
    key_list = jax.random.split(jax.random.key(seed), 8)
    queries = scatter_about(key_list[0], (SEQ, INNER), 1.0, 5.0, ((0, 128), (1, 8)))
    keys = scatter_about(key_list[1], (SEQ, INNER), 1.0, 5.0, ((0, 128), (1, 8)))
    values = draw_values(jax.random.fold_in(key_list[7], 71), 0)
    gate_logits = scatter_about(key_list[3], (SEQ, INNER), 1.5, 6.0, ((0, 128), (1, 8)))
    norm_gain = jnp.clip(1.0 + 0.18 * jax.random.normal(key_list[4], (INNER,), jnp.float32), 0.1, 1.9)
    out_weight = scatter_about(key_list[5], (INNER, D), INNER ** -0.5, 0.09375, ((1, 8),))
    residual = scatter_about(key_list[6], (SEQ, D), 0.5, 4.0, ((0, 128), (1, 8)))
    return dict(queries=queries, keys=keys, values=values, gate_logits=gate_logits, norm_gain=norm_gain, out_weight=out_weight, residual=residual)


epsilon = 1e-06

def reference(queries, keys, values, gate_logits, norm_gain, out_weight, residual):
    block_count = SEQ // BLOCK
    query_blocks = queries.reshape(block_count, BLOCK, HEADS, HEAD_DIM)
    key_blocks = keys.reshape(block_count, BLOCK, HEADS, HEAD_DIM)
    value_blocks = values.reshape(block_count, BLOCK, HEADS, HEAD_DIM)
    causal_mask = jnp.tril(jnp.ones((BLOCK, BLOCK), dtype=bool))

    def advance(state_sum, block_inputs):
        query_part, key_part, value_part = block_inputs
        query_float = query_part.astype(jnp.float32)
        key_float = key_part.astype(jnp.float32)
        value_float = value_part.astype(jnp.float32)
        scores = jnp.einsum('thd,shd->hts', query_float, key_float, precision=lax.Precision.HIGHEST)
        scores = jnp.where(causal_mask[None], scores, jnp.float32(0.0)).astype(jnp.bfloat16)
        scores = lax.optimization_barrier(scores).astype(jnp.float32)
        local_part = jnp.einsum('hts,shd->thd', scores, value_float, precision=lax.Precision.HIGHEST)
        carried_part = jnp.einsum('thd,hde->the', query_float, state_sum, precision=lax.Precision.HIGHEST)
        block_state = jnp.einsum('shd,she->hde', key_float, value_float, precision=lax.Precision.HIGHEST)
        return (state_sum + block_state, (local_part + carried_part).astype(jnp.bfloat16))
    start_state = jnp.zeros((HEADS, HEAD_DIM, HEAD_DIM), jnp.float32)
    final_state, attended = lax.scan(advance, start_state, (query_blocks, key_blocks, value_blocks))
    attended = attended.reshape(SEQ, INNER).astype(jnp.float32)
    mean_square = lax.optimization_barrier(jnp.sum(attended * attended, axis=1)) / INNER
    scale_rows = lax.rsqrt(mean_square + epsilon)
    normed = attended * scale_rows[:, None] * norm_gain[None, :] * jax.nn.sigmoid(gate_logits.astype(jnp.float32))
    normed = normed.astype(jnp.bfloat16)
    projected = jnp.dot(normed, out_weight, preferred_element_type=jnp.float32)
    return (projected + residual.astype(jnp.float32)).astype(jnp.bfloat16)
```

```python
import jax
import jax.numpy as jnp
from jax import lax
from jax.experimental import pallas as pl
from jax.experimental.pallas import tpu as pltpu
from jax.sharding import Mesh, PartitionSpec as P

HEAD_DIM = 128
BLOCK = 256
INNER = 4096
SIDE = 8
CORES = 2

epsilon = 1e-06
f32 = jnp.float32
bf16 = jnp.bfloat16


def call(kernel, out_shape, *args, flops=0, smem=0):
    size = sum(a.size * a.dtype.itemsize for a in args)
    return pl.pallas_call(
        kernel,
        out_shape=out_shape,
        in_specs=[pl.BlockSpec(memory_space=pltpu.SMEM)] * smem
        + [pl.BlockSpec(memory_space=pltpu.VMEM)] * (len(args) - smem),
        out_specs=jax.tree.map(lambda _: pl.BlockSpec(memory_space=pltpu.VMEM), out_shape),
        cost_estimate=pl.CostEstimate(flops=flops, bytes_accessed=size, transcendentals=0),
    )(*args)


def heads_of(ref):
    return [slice(h * HEAD_DIM, (h + 1) * HEAD_DIM) for h in range(ref.shape[1] // HEAD_DIM)]


def state_kernel(keys, values, out):
    rows = out.shape[1]
    per = HEAD_DIM // rows
    for h, cols in enumerate(heads_of(keys)):
        state = lax.dot_general(
            keys[:, cols], values[:, cols], (((0,), (0,)), ((), ())), preferred_element_type=f32
        )
        out[h * per : (h + 1) * per] = state.reshape(per, rows, HEAD_DIM).astype(bf16)


def total_kernel(row, out):
    total = row[0].astype(f32)
    for member in range(1, row.shape[0]):
        total = total + row[member].astype(f32)
    out[...] = jnp.broadcast_to(total.astype(bf16)[None], out.shape)


def prefix_kernel(place, row, totals, out):
    mine = place[0]
    run = jnp.zeros(row.shape[1:], f32)
    for other in range(totals.shape[0]):
        run = run + jnp.where(other < mine, totals[other].astype(f32), 0.0)
    for member in range(row.shape[0]):
        out[member] = run.astype(bf16)
        run = run + row[member].astype(f32)


def local_kernel(queries, keys, values, gates, gain, local, gated):
    tokens = queries.shape[0]
    later = lax.broadcasted_iota(jnp.int32, (tokens, tokens), 0)
    earlier = lax.broadcasted_iota(jnp.int32, (tokens, tokens), 1)
    for cols in heads_of(queries):
        scores = lax.dot_general(
            queries[:, cols], keys[:, cols], (((1,), (1,)), ((), ())), preferred_element_type=f32
        )
        scores = jnp.where(earlier <= later, scores, 0.0).astype(bf16)
        local[:, cols] = jnp.dot(scores, values[:, cols], preferred_element_type=f32)
    gated[...] = gain[...] * jax.nn.sigmoid(gates[...].astype(f32))


def attend_kernel(queries, state, local, gated, out):
    tokens = queries.shape[0]
    squares = jnp.zeros((tokens, 1), f32)
    for h, cols in enumerate(heads_of(queries)):
        part = jnp.dot(queries[:, cols], state[h], preferred_element_type=f32)
        attended = (local[:, cols] + part).astype(bf16).astype(f32)
        squares = squares + jnp.sum(attended * attended, axis=1, keepdims=True)
        out[:tokens, cols] = (attended * gated[:, cols]).astype(bf16)
    lane = lax.broadcasted_iota(jnp.int32, (tokens, HEAD_DIM), 1)
    high = squares.astype(bf16).astype(f32)
    middle = (squares - high).astype(bf16).astype(f32)
    low = squares - high - middle
    packed = jnp.where(lane == 0, high, jnp.where(lane == 1, middle, jnp.where(lane == 2, low, 0.0)))
    extra = out.shape[0] - tokens
    out[tokens:, :tokens] = packed.T[:extra].astype(bf16)
    out[tokens:, tokens:] = jnp.zeros((extra, out.shape[1] - tokens), bf16)


def exchange(blocks, axes):
    return lax.all_to_all(blocks, axes, 0, 0, tiled=True)


def shift(block, hops):
    pairs = [(place, (place + hops) % SIDE) for place in range(SIDE)]
    return lax.ppermute(block, "z", pairs)


def on_device(queries, keys, values, gate_logits, norm_gain, out_weight, residual):
    tokens, width = queries.shape
    heads = width // HEAD_DIM
    row_places = SIDE * CORES
    rows = heads * HEAD_DIM // row_places
    z = lax.axis_index("z")
    shape = jax.ShapeDtypeStruct

    own = call(
        state_kernel, shape((row_places, rows, HEAD_DIM), bf16), keys, values,
        flops=2 * tokens * width * HEAD_DIM,
    )
    row = exchange(own, ("x", "core"))
    totals = call(total_kernel, shape((SIDE, rows, HEAD_DIM), bf16), row)
    totals = exchange(totals, "y")
    place = lax.axis_index("y").reshape(1)
    state = call(
        prefix_kernel, shape((row_places, rows, HEAD_DIM), bf16), place, row, totals, smem=1
    )
    state = exchange(state, ("x", "core")).reshape(heads, HEAD_DIM, HEAD_DIM)

    gain_here = lax.dynamic_slice_in_dim(norm_gain, z * width, width, 0)[None]
    local, gated = call(
        local_kernel, [shape((tokens, width), f32)] * 2,
        queries, keys, values, gate_logits, gain_here,
        flops=4 * tokens * tokens * width,
    )
    block = call(
        attend_kernel, shape((tokens + 16, width), bf16), queries, state, local, gated,
        flops=2 * tokens * width * HEAD_DIM,
    )

    def product(piece, offset):
        source = lax.rem(z + offset + SIDE, SIDE)
        weight = lax.dynamic_slice_in_dim(out_weight, source * width, width, 0)
        return jnp.dot(piece[:tokens], weight, preferred_element_type=f32)

    def squares(piece):
        return jnp.sum(piece[tokens : tokens + 3, :tokens].astype(f32), axis=0)

    half = tokens // 2
    up1, down1 = shift(block, -1), shift(block, 1)
    up2, down2 = shift(up1, -1), shift(down1, 1)
    up3, down3 = shift(up2, -1), shift(down2, 1)
    far = jnp.concatenate([shift(up2[:half], -2), shift(down2[half:], 2)], axis=0)
    pieces = [(block, 0), (up1, 1), (down1, -1), (up2, 2), (down2, -2), (up3, 3), (down3, -3), (far, 4)]
    total = jnp.zeros((tokens,), f32)
    projected = None
    for piece, offset in pieces:
        total = total + squares(piece)
        part = product(piece, offset)
        projected = part if projected is None else projected + part
    scale_rows = lax.rsqrt(total / INNER + epsilon)
    return (projected * scale_rows[:, None] + residual.astype(f32)).astype(bf16)


def solution(mesh):
    split = Mesh(mesh.devices.reshape(SIDE, SIDE, CORES, SIDE), ("y", "x", "core", "z"))
    ctx = ("y", "x", "core")
    in_specs = (
        P(ctx, "z"),
        P(ctx, "z"),
        P(ctx, "z"),
        P(ctx, "z"),
        P(),
        P(None, "z"),
        P(ctx, "z"),
    )
    return jax.shard_map(
        on_device, mesh=split, in_specs=in_specs, out_specs=P(ctx, "z"), check_vma=False
    )
```

```python
import jax
import jax.numpy as jnp
from jax import lax
from jax.experimental import pallas as pl
from jax.experimental.pallas import tpu as pltpu
from jax.sharding import Mesh, PartitionSpec as P

HEAD_DIM = 128
BLOCK = 256
INNER = 4096
SIDE = 8
CORES = 2
LIMIT = 12 * 2**20

epsilon = 1e-06
f32 = jnp.float32
bf16 = jnp.bfloat16


def call(kernel, out_shape, *args, flops=0, smem=0):
    size = sum(a.size * a.dtype.itemsize for a in args)
    return pl.pallas_call(
        kernel,
        out_shape=out_shape,
        in_specs=[pl.BlockSpec(memory_space=pltpu.SMEM)] * smem
        + [pl.BlockSpec(memory_space=pltpu.VMEM)] * (len(args) - smem),
        out_specs=jax.tree.map(lambda _: pl.BlockSpec(memory_space=pltpu.VMEM), out_shape),
        compiler_params=pltpu.CompilerParams(vmem_limit_bytes=LIMIT),
        cost_estimate=pl.CostEstimate(flops=flops, bytes_accessed=size, transcendentals=0),
    )(*args)


def heads_of(ref):
    return [slice(h * HEAD_DIM, (h + 1) * HEAD_DIM) for h in range(ref.shape[1] // HEAD_DIM)]


def state_kernel(keys, values, out):
    rows = out.shape[1]
    per = HEAD_DIM // rows
    for h, cols in enumerate(heads_of(keys)):
        state = lax.dot_general(
            keys[:, cols], values[:, cols], (((0,), (0,)), ((), ())), preferred_element_type=f32
        )
        out[h * per : (h + 1) * per] = state.reshape(per, rows, HEAD_DIM).astype(bf16)


def total_kernel(row, out):
    total = row[0].astype(f32)
    for member in range(1, row.shape[0]):
        total = total + row[member].astype(f32)
    out[...] = jnp.broadcast_to(total.astype(bf16)[None], out.shape)


def prefix_kernel(place, row, totals, out):
    mine = place[0]
    run = jnp.zeros(row.shape[1:], f32)
    for other in range(totals.shape[0]):
        run = run + jnp.where(other < mine, totals[other].astype(f32), 0.0)
    for member in range(row.shape[0]):
        out[member] = run.astype(bf16)
        run = run + row[member].astype(f32)


def local_kernel(queries, keys, values, gates, gain, local, gated):
    tokens = queries.shape[0]
    later = lax.broadcasted_iota(jnp.int32, (tokens, tokens), 0)
    earlier = lax.broadcasted_iota(jnp.int32, (tokens, tokens), 1)
    for cols in heads_of(queries):
        scores = lax.dot_general(
            queries[:, cols], keys[:, cols], (((1,), (1,)), ((), ())), preferred_element_type=f32
        )
        scores = jnp.where(earlier <= later, scores, 0.0).astype(bf16)
        local[:, cols] = jnp.dot(scores, values[:, cols], preferred_element_type=f32)
    gated[...] = gain[...] * jax.nn.sigmoid(gates[...].astype(f32))


def attend_kernel(queries, state, local, gated, out):
    tokens = queries.shape[0]
    squares = jnp.zeros((tokens, 1), f32)
    for h, cols in enumerate(heads_of(queries)):
        part = jnp.dot(queries[:, cols], state[h], preferred_element_type=f32)
        attended = (local[:, cols] + part).astype(bf16).astype(f32)
        squares = squares + jnp.sum(attended * attended, axis=1, keepdims=True)
        out[:tokens, cols] = (attended * gated[:, cols]).astype(bf16)
    lane = lax.broadcasted_iota(jnp.int32, (tokens, HEAD_DIM), 1)
    high = squares.astype(bf16).astype(f32)
    middle = (squares - high).astype(bf16).astype(f32)
    low = squares - high - middle
    packed = jnp.where(lane == 0, high, jnp.where(lane == 1, middle, jnp.where(lane == 2, low, 0.0)))
    extra = out.shape[0] - tokens
    out[tokens:, :tokens] = packed.T[:extra].astype(bf16)
    out[tokens:, tokens:] = jnp.zeros((extra, out.shape[1] - tokens), bf16)


def exchange(blocks, axes):
    return lax.all_to_all(blocks, axes, 0, 0, tiled=True)


def hop(block):
    upward = [(z, (z + 1) % SIDE) for z in range(SIDE)]
    downward = [(SIDE + z, SIDE + (z - 1) % SIDE) for z in range(SIDE)]
    return lax.ppermute(block, ("core", "z"), upward + downward)


def swap(block):
    return lax.ppermute(block, "core", [(0, 1), (1, 0)])


def on_device(queries, keys, values, gate_logits, norm_gain, out_weight, residual):
    tokens, width = queries.shape
    heads = width // HEAD_DIM
    row_places = SIDE * CORES
    rows = heads * HEAD_DIM // row_places
    z = lax.axis_index("z")
    shape = jax.ShapeDtypeStruct

    own = call(
        state_kernel, shape((row_places, rows, HEAD_DIM), bf16), keys, values,
        flops=2 * tokens * width * HEAD_DIM,
    )
    row = exchange(own, ("x", "core"))
    totals = call(total_kernel, shape((SIDE, rows, HEAD_DIM), bf16), row)
    totals = exchange(totals, "y")
    place = lax.axis_index("y").reshape(1)
    state = call(
        prefix_kernel, shape((row_places, rows, HEAD_DIM), bf16), place, row, totals, smem=1
    )
    state = exchange(state, ("x", "core")).reshape(heads, HEAD_DIM, HEAD_DIM)

    gain_here = lax.dynamic_slice_in_dim(norm_gain, z * width, width, 0)[None]
    local, gated = call(
        local_kernel, [shape((tokens, width), f32)] * 2,
        queries, keys, values, gate_logits, gain_here,
        flops=4 * tokens * tokens * width,
    )
    block = call(
        attend_kernel, shape((tokens + 16, width), bf16), queries, state, local, gated,
        flops=2 * tokens * width * HEAD_DIM,
    )

    behind = 2 * lax.axis_index("core") - 1

    def product(piece, offset):
        source = lax.rem(z + offset * behind + SIDE, SIDE)
        weight = lax.dynamic_slice_in_dim(out_weight, source * width, width, 0)
        return jnp.dot(piece[:tokens], weight, preferred_element_type=f32)

    def squares(piece):
        return jnp.sum(piece[tokens : tokens + 3, :tokens].astype(f32), axis=0)

    mine, other = block, swap(block)
    pieces = [(block, 0)]
    for step in range(1, SIDE // 2):
        mine, other = hop(mine), hop(other)
        pieces += [(mine, step), (swap(other), -step)]
    pieces.append((hop(mine), SIDE // 2))
    total = jnp.zeros((tokens,), f32)
    projected = None
    for piece, offset in pieces:
        total = total + squares(piece)
        part = product(piece, offset)
        projected = part if projected is None else projected + part
    scale_rows = lax.rsqrt(total / INNER + epsilon)
    return (projected * scale_rows[:, None] + residual.astype(f32)).astype(bf16)


def solution(mesh):
    split = Mesh(mesh.devices.reshape(SIDE, SIDE, CORES, SIDE), ("y", "x", "core", "z"))
    ctx = ("y", "x", "core")
    in_specs = (
        P(ctx, "z"),
        P(ctx, "z"),
        P(ctx, "z"),
        P(ctx, "z"),
        P(),
        P(None, "z"),
        P(ctx, "z"),
    )
    return jax.shard_map(
        on_device, mesh=split, in_specs=in_specs, out_specs=P(ctx, "z"), check_vma=False
    )
```

```python
import jax
import jax.numpy as jnp
from jax import lax
from jax.experimental import pallas as pl
from jax.experimental.pallas import tpu as pltpu
from jax.sharding import Mesh, PartitionSpec as P

HEAD_DIM = 128
BLOCK = 256
INNER = 4096
SIDE = 8
CORES = 2
LIMIT = 12 * 2**20

epsilon = 1e-06
f32 = jnp.float32
bf16 = jnp.bfloat16


VMEM = pl.BlockSpec(memory_space=pltpu.VMEM)
SMEM = pl.BlockSpec(memory_space=pltpu.SMEM)


def call(kernel, out_shape, specs, args, flops=0):
    size = sum(a.size * a.dtype.itemsize for a in args)
    return pl.pallas_call(
        kernel,
        out_shape=out_shape,
        in_specs=specs,
        out_specs=jax.tree.map(lambda _: VMEM, out_shape),
        compiler_params=pltpu.CompilerParams(vmem_limit_bytes=LIMIT),
        cost_estimate=pl.CostEstimate(flops=flops, bytes_accessed=size, transcendentals=0),
    )(*args)


def heads_of(ref):
    return [slice(h * HEAD_DIM, (h + 1) * HEAD_DIM) for h in range(ref.shape[1] // HEAD_DIM)]


def state_kernel(keys, values, out):
    rows = out.shape[1]
    per = HEAD_DIM // rows
    for h, cols in enumerate(heads_of(keys)):
        state = lax.dot_general(
            keys[:, cols], values[:, cols], (((0,), (0,)), ((), ())), preferred_element_type=f32
        )
        out[h * per : (h + 1) * per] = state.reshape(per, rows, HEAD_DIM).astype(bf16)


def total_kernel(row, out):
    total = row[0].astype(f32)
    for member in range(1, row.shape[0]):
        total = total + row[member].astype(f32)
    out[...] = jnp.broadcast_to(total.astype(bf16)[None], out.shape)


def prefix_kernel(place, row, totals, out):
    mine = place[0]
    run = jnp.zeros(row.shape[1:], f32)
    for other in range(totals.shape[0]):
        run = run + jnp.where(other < mine, totals[other].astype(f32), 0.0)
    for member in range(row.shape[0]):
        out[member] = run.astype(bf16)
        run = run + row[member].astype(f32)


def local_kernel(queries, keys, values, local, queries_kept):
    tokens = queries.shape[0]
    later = lax.broadcasted_iota(jnp.int32, (tokens, tokens), 0)
    earlier = lax.broadcasted_iota(jnp.int32, (tokens, tokens), 1)
    for cols in heads_of(queries):
        scores = lax.dot_general(
            queries[:, cols], keys[:, cols], (((1,), (1,)), ((), ())), preferred_element_type=f32
        )
        scores = jnp.where(earlier <= later, scores, 0.0).astype(bf16)
        local[:, cols] = jnp.dot(scores, values[:, cols], preferred_element_type=f32)
    queries_kept[...] = queries[...]


def gate_kernel(place, gain, gates, gated):
    groups = heads_of(gates)
    for h, cols in enumerate(groups):
        gain_row = gain[pl.ds(place[0] * len(groups) + h, 1), :]
        gated[:, cols] = gain_row * jax.nn.sigmoid(gates[:, cols].astype(f32))


def attend_kernel(queries, state, local, gated, out):
    tokens = queries.shape[0]
    squares = jnp.zeros((tokens, 1), f32)
    for h, cols in enumerate(heads_of(queries)):
        part = jnp.dot(queries[:, cols], state[h], preferred_element_type=f32)
        attended = (local[:, cols] + part).astype(bf16).astype(f32)
        squares = squares + jnp.sum(attended * attended, axis=1, keepdims=True)
        out[:tokens, cols] = (attended * gated[:, cols]).astype(bf16)
    lane = lax.broadcasted_iota(jnp.int32, (tokens, HEAD_DIM), 1)
    high = squares.astype(bf16).astype(f32)
    middle = (squares - high).astype(bf16).astype(f32)
    low = squares - high - middle
    packed = jnp.where(lane == 0, high, jnp.where(lane == 1, middle, jnp.where(lane == 2, low, 0.0)))
    extra = out.shape[0] - tokens
    out[tokens:, :tokens] = packed.T[:extra].astype(bf16)
    out[tokens:, tokens:] = jnp.zeros((extra, out.shape[1] - tokens), bf16)


def exchange(blocks, axes):
    return lax.all_to_all(blocks, axes, 0, 0, tiled=True)


def ring(block, sign):
    pairs = [(z, (z + sign) % SIDE) for z in range(SIDE)]
    pairs += [(SIDE + z, SIDE + (z - sign) % SIDE) for z in range(SIDE)]
    return lax.ppermute(block, ("core", "z"), pairs)


def shift(block, hops):
    return lax.ppermute(block, "z", [(z, (z + hops) % SIDE) for z in range(SIDE)])


def gather_seven(block, tokens):
    one = two = block
    pieces = [(block, 0)]
    for step in range(1, SIDE // 2):
        one, two = ring(one, 1), ring(two, -1)
        pieces += [(one, step), (two, -step)]
    pieces.append((ring(one, 1), SIDE // 2))
    behind = 2 * lax.axis_index("core") - 1
    return [(piece, offset * behind) for piece, offset in pieces]


def gather_three(block, tokens):
    half = tokens // 2
    up1, down1 = shift(block, -1), shift(block, 1)
    up2, down2 = shift(up1, -1), shift(down1, 1)
    block, up1, down1, up2, down2 = lax.optimization_barrier((block, up1, down1, up2, down2))
    up3, down3 = shift(up2, -1), shift(down2, 1)
    far = jnp.concatenate([shift(up2[:half], -2), shift(down2[half:], 2)], axis=0)
    return [(block, 0), (up1, 1), (down1, -1), (up2, 2), (down2, -2), (up3, 3), (down3, -3), (far, 4)]


def finish(pieces, weight, residual):
    tokens = residual.shape[0]
    z = lax.axis_index("z")
    total = jnp.zeros((tokens,), f32)
    projected = None
    for piece, offset in pieces:
        width = piece.shape[1]
        source = lax.rem(z + offset + SIDE, SIDE)
        rows = lax.dynamic_slice_in_dim(weight, source * width, width, 0)
        part = jnp.dot(piece[:tokens], rows, preferred_element_type=f32)
        total = total + jnp.sum(piece[tokens : tokens + 3, :tokens].astype(f32), axis=0)
        projected = part if projected is None else projected + part
    scale_rows = lax.rsqrt(total / INNER + epsilon)
    return (projected * scale_rows[:, None] + residual.astype(f32)).astype(bf16)


gather = gather_three


def on_device(queries, keys, values, gate_logits, norm_gain, out_weight, residual):
    tokens, width = queries.shape
    heads = width // HEAD_DIM
    row_places = SIDE * CORES
    rows = heads * HEAD_DIM // row_places
    shape = jax.ShapeDtypeStruct
    tile = shape((tokens, width), bf16)
    wide = shape((tokens, width), f32)
    chunk = shape((row_places, rows, HEAD_DIM), bf16)

    own = call(
        state_kernel, chunk, [VMEM] * 2, (keys, values), flops=2 * tokens * width * HEAD_DIM
    )
    row = exchange(own, ("x", "core"))
    totals = call(total_kernel, shape((SIDE, rows, HEAD_DIM), bf16), [VMEM], (row,))
    totals, queries = lax.optimization_barrier((totals, queries))
    totals = exchange(totals, "y")
    local, queries = call(
        local_kernel, [wide, tile], [VMEM] * 3, (queries, keys, values),
        flops=4 * tokens * tokens * width,
    )
    y_place = lax.axis_index("y").reshape(1)
    totals, local = lax.optimization_barrier((totals, local))
    state = call(prefix_kernel, chunk, [SMEM, VMEM, VMEM], (y_place, row, totals))
    state, gate_logits = lax.optimization_barrier((state, gate_logits))
    state = exchange(state, ("x", "core")).reshape(heads, HEAD_DIM, HEAD_DIM)
    z_place = lax.axis_index("z").reshape(1)
    gated = call(
        gate_kernel, wide, [SMEM, VMEM, VMEM],
        (z_place, norm_gain.reshape(-1, HEAD_DIM), gate_logits), flops=tokens * width,
    )
    block = call(
        attend_kernel, shape((tokens + 16, width), bf16), [VMEM] * 4,
        (queries, state, local, gated), flops=2 * tokens * width * HEAD_DIM,
    )
    return finish(gather(block, tokens), out_weight, residual)


def solution(mesh):
    split = Mesh(mesh.devices.reshape(SIDE, SIDE, CORES, SIDE), ("y", "x", "core", "z"))
    ctx = ("y", "x", "core")
    in_specs = (
        P(ctx, "z"),
        P(ctx, "z"),
        P(ctx, "z"),
        P(ctx, "z"),
        P(),
        P(None, "z"),
        P(ctx, "z"),
    )
    return jax.shard_map(
        on_device, mesh=split, in_specs=in_specs, out_specs=P(ctx, "z"), check_vma=False
    )
```

```python
import jax
import jax.numpy as jnp
from jax import lax
from jax.experimental import pallas as pl
from jax.experimental.pallas import tpu as pltpu
from jax.sharding import Mesh, PartitionSpec as P

HEAD_DIM = 128
BLOCK = 256
INNER = 4096
SIDE = 8
CORES = 2
LIMIT = 12 * 2**20

epsilon = 1e-06
f32 = jnp.float32
bf16 = jnp.bfloat16


VMEM = pl.BlockSpec(memory_space=pltpu.VMEM)
SMEM = pl.BlockSpec(memory_space=pltpu.SMEM)


def call(kernel, out_shape, specs, args, flops=0):
    size = sum(a.size * a.dtype.itemsize for a in args)
    return pl.pallas_call(
        kernel,
        out_shape=out_shape,
        in_specs=specs,
        out_specs=jax.tree.map(lambda _: VMEM, out_shape),
        compiler_params=pltpu.CompilerParams(vmem_limit_bytes=LIMIT),
        cost_estimate=pl.CostEstimate(flops=flops, bytes_accessed=size, transcendentals=0),
    )(*args)


def heads_of(ref):
    return [slice(h * HEAD_DIM, (h + 1) * HEAD_DIM) for h in range(ref.shape[1] // HEAD_DIM)]


def state_kernel(keys, values, out):
    rows = out.shape[1]
    per = HEAD_DIM // rows
    for h, cols in enumerate(heads_of(keys)):
        state = lax.dot_general(
            keys[:, cols], values[:, cols], (((0,), (0,)), ((), ())), preferred_element_type=f32
        )
        out[h * per : (h + 1) * per] = state.reshape(per, rows, HEAD_DIM).astype(bf16)


def total_kernel(row, out):
    total = row[0].astype(f32)
    for member in range(1, row.shape[0]):
        total = total + row[member].astype(f32)
    out[...] = jnp.broadcast_to(total.astype(bf16)[None], out.shape)


def prefix_kernel(place, row, totals, out):
    mine = place[0]
    run = jnp.zeros(row.shape[1:], f32)
    for other in range(totals.shape[0]):
        run = run + jnp.where(other < mine, totals[other].astype(f32), 0.0)
    for member in range(row.shape[0]):
        out[member] = run.astype(bf16)
        run = run + row[member].astype(f32)


def local_kernel(queries, keys, values, local, queries_kept):
    tokens = queries.shape[0]
    later = lax.broadcasted_iota(jnp.int32, (tokens, tokens), 0)
    earlier = lax.broadcasted_iota(jnp.int32, (tokens, tokens), 1)
    for cols in heads_of(queries):
        scores = lax.dot_general(
            queries[:, cols], keys[:, cols], (((1,), (1,)), ((), ())), preferred_element_type=f32
        )
        scores = jnp.where(earlier <= later, scores, 0.0).astype(bf16)
        local[:, cols] = jnp.dot(scores, values[:, cols], preferred_element_type=f32)
    queries_kept[...] = queries[...]


def gate_kernel(place, gain, gates, gated):
    groups = heads_of(gates)
    for h, cols in enumerate(groups):
        gain_row = gain[pl.ds(place[0] * len(groups) + h, 1), :]
        gated[:, cols] = gain_row * jax.nn.sigmoid(gates[:, cols].astype(f32))


def attend_kernel(queries, state, local, gated, out):
    tokens = queries.shape[0]
    squares = jnp.zeros((tokens, 1), f32)
    for h, cols in enumerate(heads_of(queries)):
        part = jnp.dot(queries[:, cols], state[h], preferred_element_type=f32)
        attended = (local[:, cols] + part).astype(bf16).astype(f32)
        squares = squares + jnp.sum(attended * attended, axis=1, keepdims=True)
        out[:tokens, cols] = (attended * gated[:, cols]).astype(bf16)
    lane = lax.broadcasted_iota(jnp.int32, (tokens, HEAD_DIM), 1)
    high = squares.astype(bf16).astype(f32)
    middle = (squares - high).astype(bf16).astype(f32)
    low = squares - high - middle
    packed = jnp.where(lane == 0, high, jnp.where(lane == 1, middle, jnp.where(lane == 2, low, 0.0)))
    extra = out.shape[0] - tokens
    out[tokens:, :tokens] = packed.T[:extra].astype(bf16)
    out[tokens:, tokens:] = jnp.zeros((extra, out.shape[1] - tokens), bf16)


def exchange(blocks, axes):
    return lax.all_to_all(blocks, axes, 0, 0, tiled=True)


def ring(block, sign):
    pairs = [(z, (z + sign) % SIDE) for z in range(SIDE)]
    pairs += [(SIDE + z, SIDE + (z - sign) % SIDE) for z in range(SIDE)]
    return lax.ppermute(block, ("core", "z"), pairs)


def swap(block):
    return lax.ppermute(block, "core", [(0, 1), (1, 0)])


def project(block, weight, residual):
    tokens = residual.shape[0]
    width = block.shape[1]
    z = lax.axis_index("z")
    behind = 2 * lax.axis_index("core") - 1
    fence = lax.optimization_barrier

    def product(piece, offset):
        source = lax.rem(z + offset * behind + SIDE, SIDE)
        rows = lax.dynamic_slice_in_dim(weight, source * width, width, 0)
        return jnp.dot(piece[:tokens], rows, preferred_element_type=f32)

    def squares(piece):
        return jnp.sum(piece[tokens : tokens + 3, :tokens].astype(f32), axis=0)

    mine1 = ring(block, 1)
    other1 = ring(swap(block), 1)
    mine2, other2 = ring(mine1, 1), ring(other1, 1)
    mine3, other3 = ring(mine2, 1), ring(other2, 1)
    mine4 = ring(mine3, 1)

    other1, other2, other3 = fence((other1, other2, other3))
    others = [(other1, 1), (other2, 2), (other3, 3)]
    partial = sum(product(piece, offset) for piece, offset in others).astype(bf16)
    partial_squares = sum(squares(piece) for piece, _ in others)
    block, mine1, mine2, mine3, partial = fence((block, mine1, mine2, mine3, partial))
    partial, partial_squares = swap(partial), swap(partial_squares)

    own = [(block, 0), (mine1, 1), (mine2, 2), (mine3, 3), (mine4, 4)]
    projected = sum(product(piece, offset) for piece, offset in own) + partial.astype(f32)
    total = sum(squares(piece) for piece, _ in own) + partial_squares
    scale_rows = lax.rsqrt(total / INNER + epsilon)
    return (projected * scale_rows[:, None] + residual.astype(f32)).astype(bf16)


def on_device(queries, keys, values, gate_logits, norm_gain, out_weight, residual):
    tokens, width = queries.shape
    heads = width // HEAD_DIM
    row_places = SIDE * CORES
    rows = heads * HEAD_DIM // row_places
    shape = jax.ShapeDtypeStruct
    tile = shape((tokens, width), bf16)
    wide = shape((tokens, width), f32)
    chunk = shape((row_places, rows, HEAD_DIM), bf16)

    own = call(
        state_kernel, chunk, [VMEM] * 2, (keys, values), flops=2 * tokens * width * HEAD_DIM
    )
    row = exchange(own, ("x", "core"))
    totals = call(total_kernel, shape((SIDE, rows, HEAD_DIM), bf16), [VMEM], (row,))
    totals, queries = lax.optimization_barrier((totals, queries))
    totals = exchange(totals, "y")
    local, queries = call(
        local_kernel, [wide, tile], [VMEM] * 3, (queries, keys, values),
        flops=4 * tokens * tokens * width,
    )
    y_place = lax.axis_index("y").reshape(1)
    totals, local = lax.optimization_barrier((totals, local))
    state = call(prefix_kernel, chunk, [SMEM, VMEM, VMEM], (y_place, row, totals))
    state, gate_logits = lax.optimization_barrier((state, gate_logits))
    state = exchange(state, ("x", "core")).reshape(heads, HEAD_DIM, HEAD_DIM)
    z_place = lax.axis_index("z").reshape(1)
    gated = call(
        gate_kernel, wide, [SMEM, VMEM, VMEM],
        (z_place, norm_gain.reshape(-1, HEAD_DIM), gate_logits), flops=tokens * width,
    )
    block = call(
        attend_kernel, shape((tokens + 16, width), bf16), [VMEM] * 4,
        (queries, state, local, gated), flops=2 * tokens * width * HEAD_DIM,
    )
    return project(block, out_weight, residual)


def solution(mesh):
    split = Mesh(mesh.devices.reshape(SIDE, SIDE, CORES, SIDE), ("y", "x", "core", "z"))
    ctx = ("y", "x", "core")
    in_specs = (
        P(ctx, "z"),
        P(ctx, "z"),
        P(ctx, "z"),
        P(ctx, "z"),
        P(),
        P(None, "z"),
        P(ctx, "z"),
    )
    return jax.shard_map(
        on_device, mesh=split, in_specs=in_specs, out_specs=P(ctx, "z"), check_vma=False
    )
```

```python
import jax
import jax.numpy as jnp
from jax import lax
from jax.experimental import pallas as pl
from jax.experimental.pallas import tpu as pltpu
from jax.sharding import Mesh, PartitionSpec as P

HEAD_DIM = 128
INNER = 4096
SIDE = 8
CORES = 2
EXTRA = 16
LIMIT = 12 * 2**20
MOST = 48 * 2**20
ALL = (60 * 1024 - 192) * 2**10

epsilon = 1e-06
f32 = jnp.float32
bf16 = jnp.bfloat16


VMEM = pl.BlockSpec(memory_space=pltpu.VMEM)
SMEM = pl.BlockSpec(memory_space=pltpu.SMEM)


ANY = pl.BlockSpec(memory_space=pl.ANY)


def call(kernel, out_shape, specs, args, scratch=(), flops=0, limit=LIMIT):
    size = sum(a.size * a.dtype.itemsize for a in args)
    return pl.pallas_call(
        kernel,
        out_shape=out_shape,
        in_specs=specs,
        out_specs=jax.tree.map(lambda _: VMEM, out_shape),
        scratch_shapes=scratch,
        compiler_params=pltpu.CompilerParams(vmem_limit_bytes=limit),
        cost_estimate=pl.CostEstimate(flops=flops, bytes_accessed=size, transcendentals=0),
    )(*args)


def heads_of(ref):
    return [slice(h * HEAD_DIM, (h + 1) * HEAD_DIM) for h in range(ref.shape[1] // HEAD_DIM)]


def state_kernel(keys_hbm, values_hbm, out, keys, values, semaphores):
    copies = [
        pltpu.make_async_copy(keys_hbm, keys, semaphores.at[0]),
        pltpu.make_async_copy(values_hbm, values, semaphores.at[1]),
    ]
    for copy in copies:
        copy.start()
    for copy in copies:
        copy.wait()
    rows = out.shape[1]
    per = HEAD_DIM // rows
    for h, cols in enumerate(heads_of(keys)):
        state = lax.dot_general(
            keys[:, cols], values[:, cols], (((0,), (0,)), ((), ())), preferred_element_type=f32
        )
        out[h * per : (h + 1) * per] = state.reshape(per, rows, HEAD_DIM).astype(bf16)


def total_kernel(row, out):
    total = row[0].astype(f32)
    for member in range(1, row.shape[0]):
        total = total + row[member].astype(f32)
    out[...] = jnp.broadcast_to(total.astype(bf16)[None], out.shape)


def prefix_kernel(place, row, totals, out):
    mine = place[0]
    run = jnp.zeros(row.shape[1:], f32)
    for other in range(totals.shape[0]):
        run = run + jnp.where(other < mine, totals[other].astype(f32), 0.0)
    for member in range(row.shape[0]):
        out[member] = run.astype(bf16)
        run = run + row[member].astype(f32)


def local_kernel(queries, keys, values, local, queries_kept):
    tokens = queries.shape[0]
    later = lax.broadcasted_iota(jnp.int32, (tokens, tokens), 0)
    earlier = lax.broadcasted_iota(jnp.int32, (tokens, tokens), 1)
    for cols in heads_of(queries):
        scores = lax.dot_general(
            queries[:, cols], keys[:, cols], (((1,), (1,)), ((), ())), preferred_element_type=f32
        )
        scores = jnp.where(earlier <= later, scores, 0.0).astype(bf16)
        local[:, cols] = jnp.dot(scores, values[:, cols], preferred_element_type=f32)
    queries_kept[...] = queries[...]


def gate_kernel(place, gain, gates, gated):
    groups = heads_of(gates)
    for h, cols in enumerate(groups):
        gain_row = gain[pl.ds(place[0] * len(groups) + h, 1), :]
        gated[:, cols] = gain_row * jax.nn.sigmoid(gates[:, cols].astype(f32))


def attend_kernel(queries, state, local, gated, out):
    tokens = queries.shape[0]
    squares = jnp.zeros((tokens, 1), f32)
    for h, cols in enumerate(heads_of(queries)):
        part = jnp.dot(queries[:, cols], state[h], preferred_element_type=f32)
        attended = (local[:, cols] + part).astype(bf16).astype(f32)
        squares = squares + jnp.sum(attended * attended, axis=1, keepdims=True)
        out[:tokens, cols] = (attended * gated[:, cols]).astype(bf16)
    lane = lax.broadcasted_iota(jnp.int32, (tokens, HEAD_DIM), 1)
    high = squares.astype(bf16).astype(f32)
    middle = (squares - high).astype(bf16).astype(f32)
    low = squares - high - middle
    packed = jnp.where(lane == 0, high, jnp.where(lane == 1, middle, jnp.where(lane == 2, low, 0.0)))
    extra = out.shape[0] - tokens
    out[tokens:, :tokens] = packed.T[:extra].astype(bf16)
    out[tokens:, tokens:] = jnp.zeros((extra, out.shape[1] - tokens), bf16)


def fetch(places, weight, buffers, semaphores):
    copies = []
    for n, buffer in enumerate(buffers):
        width = buffer.shape[0]
        rows = weight.at[pl.ds(places[n] * width, width), :]
        copies.append(pltpu.make_async_copy(rows, buffer, semaphores.at[n]))
        copies[-1].start()
    return copies


def accumulate(pieces, copies, buffers, tokens):
    total = None
    squares = jnp.zeros((1, tokens), f32)
    for piece, copy, buffer in zip(pieces, copies, buffers):
        extra = piece[tokens:, :tokens].astype(f32)
        squares = squares + jnp.sum(extra[:3], axis=0, keepdims=True)
        copy.wait()
        part = jnp.dot(piece[:tokens], buffer[...], preferred_element_type=f32)
        total = part if total is None else total + part
    return total, squares


def other_kernel(places, one, two, three, weight, out, rows, semaphores):
    tokens = one.shape[0] - EXTRA
    buffers = [rows.at[n] for n in range(3)]
    copies = fetch(places, weight, buffers, semaphores)
    total, squares = accumulate([one, two, three], copies, buffers, tokens)
    out[:tokens] = total.astype(bf16)
    high = squares.astype(bf16).astype(f32)
    middle = (squares - high).astype(bf16).astype(f32)
    low = squares - high - middle
    extra = out.shape[0] - tokens
    place = lax.broadcasted_iota(jnp.int32, (extra, tokens), 0)
    packed = jnp.where(place == 0, high, jnp.where(place == 1, middle, jnp.where(place == 2, low, 0.0)))
    out[tokens:, :tokens] = packed.astype(bf16)
    out[tokens:, tokens:] = jnp.zeros((extra, out.shape[1] - tokens), bf16)


def own_kernel(places, block, one, two, three, weight, out, squares_out, last, rows, semaphores):
    tokens = out.shape[0]
    buffers = [rows.at[n] for n in range(4)]
    copies = fetch(places, weight, buffers + [last], semaphores)
    total, squares = accumulate([block, one, two, three], copies[:4], buffers, tokens)
    out[...] = total
    squares_out[...] = jnp.broadcast_to(squares, squares_out.shape)
    copies[4].wait()


def exchange(blocks, axes):
    return lax.all_to_all(blocks, axes, 0, 0, tiled=True)


def ring(block, sign):
    pairs = [(z, (z + sign) % SIDE) for z in range(SIDE)]
    pairs += [(SIDE + z, SIDE + (z - sign) % SIDE) for z in range(SIDE)]
    return lax.ppermute(block, ("core", "z"), pairs)


def swap(block):
    return lax.ppermute(block, "core", [(0, 1), (1, 0)])


def project(block, weight, residual):
    tokens, columns = residual.shape
    width = block.shape[1]
    z = lax.axis_index("z")
    behind = 2 * lax.axis_index("core") - 1
    fence = lax.optimization_barrier
    shape = jax.ShapeDtypeStruct

    def source(offset):
        return lax.rem(z + offset * behind + SIDE, SIDE)

    def places(offsets):
        return jnp.stack([source(offset) for offset in offsets])

    mine1 = ring(block, 1)
    other1 = ring(swap(block), 1)
    mine2, other2 = ring(mine1, 1), ring(other1, 1)
    mine3, other3 = ring(mine2, 1), ring(other2, 1)
    mine4 = ring(mine3, 1)

    partial = call(
        other_kernel, shape((block.shape[0], columns), bf16), [SMEM] + [VMEM] * 3 + [ANY],
        (places([1, 2, 3]), other1, other2, other3, weight),
        [pltpu.VMEM((3, width, columns), bf16), pltpu.SemaphoreType.DMA((3,))],
        flops=6 * tokens * width * columns, limit=MOST,
    )
    block, mine1, mine2, mine3, partial = fence((block, mine1, mine2, mine3, partial))
    partial = swap(partial)
    projected, squares, last = call(
        own_kernel,
        [shape((tokens, columns), f32), shape((8, tokens), f32), shape((width, columns), bf16)],
        [SMEM] + [VMEM] * 4 + [ANY],
        (places([0, 1, 2, 3, 4]), block, mine1, mine2, mine3, weight),
        [pltpu.VMEM((4, width, columns), bf16), pltpu.SemaphoreType.DMA((5,))],
        flops=8 * tokens * width * columns, limit=MOST,
    )

    def squares_of(piece):
        return jnp.sum(piece[tokens : tokens + 3, :tokens].astype(f32), axis=0)

    projected = projected + jnp.dot(mine4[:tokens], last, preferred_element_type=f32)
    projected = projected + partial[:tokens].astype(f32)
    total = squares[0] + squares_of(partial) + squares_of(mine4)
    scale_rows = lax.rsqrt(total / INNER + epsilon)
    return (projected * scale_rows[:, None] + residual.astype(f32)).astype(bf16)


def on_device(queries, keys, values, gate_logits, norm_gain, out_weight, residual):
    tokens, width = queries.shape
    heads = width // HEAD_DIM
    row_places = SIDE * CORES
    rows = heads * HEAD_DIM // row_places
    shape = jax.ShapeDtypeStruct
    tile = shape((tokens, width), bf16)
    wide = shape((tokens, width), f32)
    chunk = shape((row_places, rows, HEAD_DIM), bf16)

    own = call(
        state_kernel, chunk, [ANY] * 2, (keys, values),
        [pltpu.VMEM((tokens, width), bf16)] * 2 + [pltpu.SemaphoreType.DMA((2,))],
        flops=2 * tokens * width * HEAD_DIM, limit=ALL,
    )
    row = exchange(own, ("x", "core"))
    totals = call(total_kernel, shape((SIDE, rows, HEAD_DIM), bf16), [VMEM], (row,))
    totals, gate_logits = lax.optimization_barrier((totals, gate_logits))
    totals = exchange(totals, "y")
    z_place = lax.axis_index("z").reshape(1)
    gated = call(
        gate_kernel, wide, [SMEM, VMEM, VMEM],
        (z_place, norm_gain.reshape(-1, HEAD_DIM), gate_logits), flops=tokens * width,
    )
    totals, gated = lax.optimization_barrier((totals, gated))
    y_place = lax.axis_index("y").reshape(1)
    state = call(prefix_kernel, chunk, [SMEM, VMEM, VMEM], (y_place, row, totals))
    state, queries = lax.optimization_barrier((state, queries))
    state = exchange(state, ("x", "core")).reshape(heads, HEAD_DIM, HEAD_DIM)
    local, queries = call(
        local_kernel, [wide, tile], [VMEM] * 3, (queries, keys, values),
        flops=4 * tokens * tokens * width,
    )
    block = call(
        attend_kernel, shape((tokens + EXTRA, width), bf16), [VMEM] * 4,
        (queries, state, local, gated), flops=2 * tokens * width * HEAD_DIM,
    )
    return project(block, out_weight, residual)


def solution(mesh):
    split = Mesh(mesh.devices.reshape(SIDE, SIDE, CORES, SIDE), ("y", "x", "core", "z"))
    ctx = ("y", "x", "core")
    in_specs = (
        P(ctx, "z"),
        P(ctx, "z"),
        P(ctx, "z"),
        P(ctx, "z"),
        P(),
        P(None, "z"),
        P(ctx, "z"),
    )
    return jax.shard_map(
        on_device, mesh=split, in_specs=in_specs, out_specs=P(ctx, "z"), check_vma=False
    )
```

```python
import jax
import jax.numpy as jnp
from jax import lax
from jax.experimental import pallas as pl
from jax.experimental.pallas import tpu as pltpu
from jax.sharding import Mesh, PartitionSpec as P

HEAD_DIM = 128
INNER = 4096
SIDE = 8
CORES = 2
EXTRA = 8
LIMIT = 12 * 2**20
MOST = 48 * 2**20
ALL = (60 * 1024 - 192) * 2**10

epsilon = 1e-06
f32 = jnp.float32
bf16 = jnp.bfloat16


VMEM = pl.BlockSpec(memory_space=pltpu.VMEM)
SMEM = pl.BlockSpec(memory_space=pltpu.SMEM)


ANY = pl.BlockSpec(memory_space=pl.ANY)


def call(kernel, out_shape, specs, args, scratch=(), flops=0, limit=LIMIT):
    size = sum(a.size * a.dtype.itemsize for a in args)
    return pl.pallas_call(
        kernel,
        out_shape=out_shape,
        in_specs=specs,
        out_specs=jax.tree.map(lambda _: VMEM, out_shape),
        scratch_shapes=scratch,
        compiler_params=pltpu.CompilerParams(vmem_limit_bytes=limit),
        cost_estimate=pl.CostEstimate(flops=flops, bytes_accessed=size, transcendentals=0),
    )(*args)


def heads_of(ref):
    return [slice(h * HEAD_DIM, (h + 1) * HEAD_DIM) for h in range(ref.shape[1] // HEAD_DIM)]


def state_kernel(keys_hbm, values_hbm, out, keys, values, semaphores):
    copies = [
        pltpu.make_async_copy(keys_hbm, keys, semaphores.at[0]),
        pltpu.make_async_copy(values_hbm, values, semaphores.at[1]),
    ]
    for copy in copies:
        copy.start()
    for copy in copies:
        copy.wait()
    rows = out.shape[1]
    per = HEAD_DIM // rows
    for h, cols in enumerate(heads_of(keys)):
        state = lax.dot_general(
            keys[:, cols], values[:, cols], (((0,), (0,)), ((), ())), preferred_element_type=f32
        )
        out[h * per : (h + 1) * per] = state.reshape(per, rows, HEAD_DIM).astype(bf16)


def total_kernel(row, out):
    total = row[0].astype(f32)
    for member in range(1, row.shape[0]):
        total = total + row[member].astype(f32)
    out[...] = jnp.broadcast_to(total.astype(bf16)[None], out.shape)


def prefix_kernel(place, row, totals, out):
    mine = place[0]
    run = jnp.zeros(row.shape[1:], f32)
    for other in range(totals.shape[0]):
        run = run + jnp.where(other < mine, totals[other].astype(f32), 0.0)
    for member in range(row.shape[0]):
        out[member] = run.astype(bf16)
        run = run + row[member].astype(f32)


def local_kernel(queries, keys, values, local, queries_kept):
    tokens = queries.shape[0]
    later = lax.broadcasted_iota(jnp.int32, (tokens, tokens), 0)
    earlier = lax.broadcasted_iota(jnp.int32, (tokens, tokens), 1)
    for cols in heads_of(queries):
        scores = lax.dot_general(
            queries[:, cols], keys[:, cols], (((1,), (1,)), ((), ())), preferred_element_type=f32
        )
        scores = jnp.where(earlier <= later, scores, 0.0).astype(bf16)
        local[:, cols] = jnp.dot(scores, values[:, cols], preferred_element_type=f32)
    queries_kept[...] = queries[...]


def rows_kernel(places, weight, rows, semaphores):
    copies = []
    for n in range(rows.shape[0]):
        width = rows.shape[1]
        source = weight.at[pl.ds(places[n] * width, width), :]
        copies.append(pltpu.make_async_copy(source, rows.at[n], semaphores.at[n]))
        copies[-1].start()
    for copy in copies:
        copy.wait()


def gate_kernel(place, gain, gates, gated):
    groups = heads_of(gates)
    for h, cols in enumerate(groups):
        gain_row = gain[pl.ds(place[0] * len(groups) + h, 1), :]
        gated[:, cols] = gain_row * jax.nn.sigmoid(gates[:, cols].astype(f32))


def attend_kernel(queries, state, local, gated, out):
    tokens = queries.shape[0]
    squares = jnp.zeros((tokens, 1), f32)
    for h, cols in enumerate(heads_of(queries)):
        part = jnp.dot(queries[:, cols], state[h], preferred_element_type=f32)
        attended = (local[:, cols] + part).astype(bf16).astype(f32)
        squares = squares + jnp.sum(attended * attended, axis=1, keepdims=True)
        out[:tokens, cols] = (attended * gated[:, cols]).astype(bf16)
    lane = lax.broadcasted_iota(jnp.int32, (tokens, HEAD_DIM), 1)
    high = squares.astype(bf16).astype(f32)
    middle = (squares - high).astype(bf16).astype(f32)
    low = squares - high - middle
    packed = jnp.where(lane == 0, high, jnp.where(lane == 1, middle, jnp.where(lane == 2, low, 0.0)))
    extra = out.shape[0] - tokens
    out[tokens:, :tokens] = packed.T[:extra].astype(bf16)
    out[tokens:, tokens:] = jnp.zeros((extra, out.shape[1] - tokens), bf16)


def accumulate(pieces, rows, first, tokens):
    total = None
    squares = jnp.zeros((1, tokens), f32)
    for n, piece in enumerate(pieces):
        extra = piece[tokens:, :tokens].astype(f32)
        squares = squares + jnp.sum(extra[:3], axis=0, keepdims=True)
        part = jnp.dot(piece[:tokens], rows[first + n], preferred_element_type=f32)
        total = part if total is None else total + part
    return total, squares


def other_kernel(one, two, three, rows, out):
    tokens = one.shape[0] - EXTRA
    total, squares = accumulate([one, two, three], rows, 1, tokens)
    out[:tokens] = total.astype(bf16)
    high = squares.astype(bf16).astype(f32)
    middle = (squares - high).astype(bf16).astype(f32)
    low = squares - high - middle
    extra = out.shape[0] - tokens
    place = lax.broadcasted_iota(jnp.int32, (extra, tokens), 0)
    packed = jnp.where(place == 0, high, jnp.where(place == 1, middle, jnp.where(place == 2, low, 0.0)))
    out[tokens:, :tokens] = packed.astype(bf16)
    out[tokens:, tokens:] = jnp.zeros((extra, out.shape[1] - tokens), bf16)


def own_kernel(block, one, two, three, rows, out, squares_out):
    tokens = out.shape[0]
    total, squares = accumulate([block, one, two, three], rows, 0, tokens)
    out[...] = total
    squares_out[...] = jnp.broadcast_to(squares, squares_out.shape)


def exchange(blocks, axes):
    return lax.all_to_all(blocks, axes, 0, 0, tiled=True)


def ring(block, sign):
    pairs = [(z, (z + sign) % SIDE) for z in range(SIDE)]
    pairs += [(SIDE + z, SIDE + (z - sign) % SIDE) for z in range(SIDE)]
    return lax.ppermute(block, ("core", "z"), pairs)


def swap(block):
    return lax.ppermute(block, "core", [(0, 1), (1, 0)])


def weight_places():
    z = lax.axis_index("z")
    behind = 2 * lax.axis_index("core") - 1
    return jnp.stack([lax.rem(z + hops * behind + SIDE, SIDE) for hops in range(SIDE // 2 + 1)])


def project(block, weight, residual):
    tokens, columns = residual.shape
    width = block.shape[1]
    fence = lax.optimization_barrier
    shape = jax.ShapeDtypeStruct

    mine1 = ring(block, 1)
    other = swap(block)
    other1 = ring(other, 1)
    places = weight_places()
    weight_rows = (places.shape[0], width, columns)
    rows = call(
        rows_kernel, shape(weight_rows, bf16), [SMEM, ANY], (places, weight),
        [pltpu.SemaphoreType.DMA((weight_rows[0],))], limit=MOST,
    )
    mine2, other2 = ring(mine1, 1), ring(other1, 1)
    mine3, other3 = ring(mine2, 1), ring(other2, 1)
    mine4 = ring(mine3, 1)

    partial = call(
        other_kernel, shape((block.shape[0], columns), bf16), [VMEM] * 4,
        (other1, other2, other3, rows), flops=6 * tokens * width * columns,
    )
    block, mine1, mine2, mine3, partial = fence((block, mine1, mine2, mine3, partial))
    partial = swap(partial)
    projected, squares = call(
        own_kernel, [shape((tokens, columns), f32), shape((8, tokens), f32)], [VMEM] * 5,
        (block, mine1, mine2, mine3, rows), flops=8 * tokens * width * columns,
    )

    def squares_of(piece):
        return jnp.sum(piece[tokens : tokens + 3, :tokens].astype(f32), axis=0)

    projected = projected + jnp.dot(mine4[:tokens], rows[-1], preferred_element_type=f32)
    projected = projected + partial[:tokens].astype(f32)
    total = squares[0] + squares_of(partial) + squares_of(mine4)
    scale_rows = lax.rsqrt(total / INNER + epsilon)
    return (projected * scale_rows[:, None] + residual.astype(f32)).astype(bf16)


def on_device(queries, keys, values, gate_logits, norm_gain, out_weight, residual):
    tokens, width = queries.shape
    heads = width // HEAD_DIM
    row_places = SIDE * CORES
    rows = heads * HEAD_DIM // row_places
    shape = jax.ShapeDtypeStruct
    tile = shape((tokens, width), bf16)
    wide = shape((tokens, width), f32)
    chunk = shape((row_places, rows, HEAD_DIM), bf16)

    own = call(
        state_kernel, chunk, [ANY] * 2, (keys, values),
        [pltpu.VMEM((tokens, width), bf16)] * 2 + [pltpu.SemaphoreType.DMA((2,))],
        flops=2 * tokens * width * HEAD_DIM, limit=ALL,
    )
    row = exchange(own, ("x", "core"))
    totals = call(total_kernel, shape((SIDE, rows, HEAD_DIM), bf16), [VMEM], (row,))
    totals, gate_logits = lax.optimization_barrier((totals, gate_logits))
    totals = exchange(totals, "y")
    z_place = lax.axis_index("z").reshape(1)
    gated = call(
        gate_kernel, wide, [SMEM, VMEM, VMEM],
        (z_place, norm_gain.reshape(-1, HEAD_DIM), gate_logits), flops=tokens * width,
    )
    totals, gated = lax.optimization_barrier((totals, gated))
    y_place = lax.axis_index("y").reshape(1)
    state = call(prefix_kernel, chunk, [SMEM, VMEM, VMEM], (y_place, row, totals))
    state, queries = lax.optimization_barrier((state, queries))
    state = exchange(state, ("x", "core")).reshape(heads, HEAD_DIM, HEAD_DIM)
    local, queries = call(
        local_kernel, [wide, tile], [VMEM] * 3, (queries, keys, values),
        flops=4 * tokens * tokens * width,
    )
    block = call(
        attend_kernel, shape((tokens + EXTRA, width), bf16), [VMEM] * 4,
        (queries, state, local, gated), flops=2 * tokens * width * HEAD_DIM,
    )
    return project(block, out_weight, residual)


def solution(mesh):
    split = Mesh(mesh.devices.reshape(SIDE, SIDE, CORES, SIDE), ("y", "x", "core", "z"))
    ctx = ("y", "x", "core")
    in_specs = (
        P(ctx, "z"),
        P(ctx, "z"),
        P(ctx, "z"),
        P(ctx, "z"),
        P(),
        P(None, "z"),
        P(ctx, "z"),
    )
    return jax.shard_map(
        on_device, mesh=split, in_specs=in_specs, out_specs=P(ctx, "z"), check_vma=False
    )
```
